32 devices in a mesh: row: 8 (over y, x, core), col: 4 (over z).
Axes of the slice: x: 2, y: 2, z: 4, core: 2. Of those that a mesh axis runs over, the one named last changes fastest.
Arguments:
- fixed_matrix_encodings: int32 [8192, 53248], P('row', 'col'), may hold values from 0 to 254, as said below
- line_restore_multiplier: float32 [8192], P('row'), may hold values from 0.001 to 0.01
- central_up_matrix: float32 [8192, 16], P('row', 'col'), may hold values from -1.5 to 1.5
- central_down_matrix: float32 [16, 53248], P('row', 'col'), may hold values from -1.5 to 1.5
- running_mean_up: float32 [8192, 16], P('row', 'col'), may hold values from -1.8 to 1.8
- squared_average_up: float32 [8192, 16], P('row', 'col'), may hold values from 0.05 to 0.5
- running_mean_down: float32 [16, 53248], P('row', 'col'), may hold values from -1.8 to 1.8
- squared_average_down: float32 [16, 53248], P('row', 'col'), may hold values from 0.05 to 0.5
- participant_change_up: bfloat16 [32, 8192, 16], P(('row', 'col')), may hold values from -48 to 48
- participant_change_down: bfloat16 [32, 16, 53248], P(('row', 'col')), may hold values from -48 to 48
- client_tallies: int32 [32, 2], P(('row', 'col')), may hold values from 1 to 64
Outputs:
- combined_normalized_entries: bfloat16 [8192, 53248], P('row', 'col')
- fresh_line_multipliers: float32 [8192], P('row')
- lora_b_next: float32 [8192, 16], P('row', 'col')
- lora_a_next: float32 [16, 53248], P('row', 'col')
- moment_b_next: float32 [8192, 16], P('row', 'col')
- second_b_next: float32 [8192, 16], P('row', 'col')
- moment_a_next: float32 [16, 53248], P('row', 'col')
- second_a_next: float32 [16, 53248], P('row', 'col')
The draws below stay inside these ranges and needn't reach their ends.
Inputs may be any that keep to these rules, and one draw needn't show every extreme that they name: `fixed_matrix_encodings`: FP8 e4m3 bit patterns; the not-a-number patterns 127 and 255 never occur.
All inputs are finite; a program needn't handle non-finite values. Where the reference program divides by a largest or mean magnitude, that divisor is 1e-20 or more.
Results may differ from the reference program's by a relative error of at most 0.0053.
Values may be sent and summed in bfloat16 or wider, within the bound.
A program may use at most 192 MiB of HBM per device.

```python
import math
import jax
import jax.numpy as jnp
from jax import lax

EMBED_SPAN = 8192
INNER_NEURONS = 53248
ADAPT_DIMENSION = 16
PARTICIPANTS = 32


def draw_fixed_matrix_encodings(key, part):
    raw = jax.random.randint(key, (EMBED_SPAN, INNER_NEURONS), 0, 254)
    return raw + (raw >= 127).astype(jnp.int32)


def draw_client_tallies(key, part):
    base = jax.random.randint(key, (PARTICIPANTS, 2), 1, 23)
    ramp = 42 * jnp.arange(PARTICIPANTS, dtype=jnp.int32) // max(PARTICIPANTS - 1, 1)
    return base + ramp[:, None]


def spiked(drawn, stream_key, source, target, shards_of, factor):
    def block_of(axis_at):
        return (jnp.arange(drawn.shape[axis_at]) // (drawn.shape[axis_at] // shards_of)).reshape((-1,) + (1,) * (drawn.ndim - 1 - axis_at))

    one_side = jax.random.permutation(stream_key, shards_of)[block_of(target)]
    other_side = (block_of(target) + shards_of // 2) % shards_of
    return jnp.where((block_of(source) == one_side) | (block_of(source) == other_side), factor * drawn, drawn)


def block_scale(key, extent, cuts, smallest, high):
    def one(position, blocks):
        heights = jax.random.uniform(jax.random.fold_in(jax.random.fold_in(key, 6), position), (blocks,), jnp.float32, smallest / len(cuts), high / len(cuts))
        return jnp.repeat(jnp.exp(heights), extent[position] // blocks).reshape((-1,) + (1,) * (len(extent) - position - 1))

    factor_of = one(*cuts[0])
    for cut in cuts[1:]:
        factor_of = factor_of * one(*cut)
    return factor_of


def scatter_about(own_key, shape, spread, limit, shards=(), kind=jnp.bfloat16):
    drawn = spread * jax.random.normal(own_key, shape, jnp.float32)
    if shards:
        drawn = drawn * block_scale(own_key, shape, shards, -0.22, 0.18)
    return jnp.clip(drawn, -limit, limit).astype(kind)


def bell_draw_with(key, extent, width, reach, split, heavy, kind=jnp.bfloat16):
    values = width * jax.random.normal(key, extent, jnp.float32)
    if split:
        values = values * block_scale(key, extent, split, -0.22, 0.18)
    return jnp.clip(spiked(values, jax.random.fold_in(key, 3), *heavy), -reach, reach).astype(kind)


def setup_inputs(seed: int = 0) -> dict:
    splits = jax.random.split(jax.random.key(seed), 12)
    return {
        "fixed_matrix_encodings": draw_fixed_matrix_encodings(jax.random.fold_in(splits[11], 71), 0),
        "line_restore_multiplier": jnp.clip(jnp.exp(math.log(0.01) - 2.30258502 * jax.random.uniform(splits[1], (EMBED_SPAN,), jnp.float32) ** block_scale(splits[1], (EMBED_SPAN,), ((0, 8),), -0.2, 0.2)), 0.001, 0.01),
        "central_up_matrix": scatter_about(splits[2], (EMBED_SPAN, ADAPT_DIMENSION), 0.25, 1.5, ((0, 8), (1, 4)), jnp.float32),
        "central_down_matrix": scatter_about(splits[3], (ADAPT_DIMENSION, INNER_NEURONS), 0.25, 1.5, ((0, 8), (1, 4)), jnp.float32),
        "running_mean_up": scatter_about(splits[4], (EMBED_SPAN, ADAPT_DIMENSION), 0.3, 1.8, ((0, 8), (1, 4)), jnp.float32),
        "squared_average_up": jnp.clip(jnp.exp(math.log(0.5) - 2.3025851 * jax.random.uniform(splits[5], (EMBED_SPAN, ADAPT_DIMENSION), jnp.float32) ** block_scale(splits[5], (EMBED_SPAN, ADAPT_DIMENSION), ((0, 8), (1, 4)), -0.2, 0.2)), 0.05, 0.5),
        "running_mean_down": scatter_about(splits[6], (ADAPT_DIMENSION, INNER_NEURONS), 0.3, 1.8, ((0, 8), (1, 4)), jnp.float32),
        "squared_average_down": jnp.clip(jnp.exp(math.log(0.5) - 2.3025851 * jax.random.uniform(splits[7], (ADAPT_DIMENSION, INNER_NEURONS), jnp.float32) ** block_scale(splits[7], (ADAPT_DIMENSION, INNER_NEURONS), ((0, 8), (1, 4)), -0.2, 0.2)), 0.05, 0.5),
        "participant_change_up": bell_draw_with(splits[8], (PARTICIPANTS, EMBED_SPAN, ADAPT_DIMENSION), 8.0, 48.0, ((0, 32),), (0, 1, 32, 2.75)),
        "participant_change_down": bell_draw_with(splits[9], (PARTICIPANTS, ADAPT_DIMENSION, INNER_NEURONS), 8.0, 48.0, ((0, 32),), (0, 2, 32, 2.75)),
        "client_tallies": draw_client_tallies(jax.random.fold_in(splits[11], 71), 0),
    }


first_decay = 0.9
second_decay = 0.99
server_rate = 0.1
adam_floor = 0.001
adapter_scale = 2.0
count_scale = 64.0
fp8_top = 448.0
peak_eps = 1e-06

def decode(codes):
    sign_bit = codes // 128
    exponent = codes // 8 % 16
    mantissa = codes % 8
    gaussian_sample = (8 + mantissa).astype(jnp.float32) * jnp.exp2((exponent - 10).astype(jnp.float32))
    subnormal = mantissa.astype(jnp.float32) * 2.0 ** (-9)
    magnitude = jnp.where(exponent > 0, gaussian_sample, subnormal)
    return magnitude * (1.0 - 2.0 * sign_bit.astype(jnp.float32))

def adaptive_update(param, moment, second, grad):
    moment_next = first_decay * moment + (1.0 - first_decay) * grad
    second_next = second_decay * second + (1.0 - second_decay) * grad * grad
    param_next = param - server_rate * moment_next / (jnp.sqrt(second_next) + adam_floor)
    return (param_next, moment_next, second_next)

def reference(fixed_matrix_encodings, line_restore_multiplier, central_up_matrix, central_down_matrix, running_mean_up, squared_average_up, running_mean_down, squared_average_down, participant_change_up, participant_change_down, client_tallies):
    weights = client_tallies.astype(jnp.float32) / (count_scale * PARTICIPANTS)
    gradient_b = lax.optimization_barrier(jnp.sum(weights[:, 0, None, None] * participant_change_up.astype(jnp.float32), axis=0))
    gradient_a = lax.optimization_barrier(jnp.sum(weights[:, 1, None, None] * participant_change_down.astype(jnp.float32), axis=0))
    updated_factor_b, updated_moment_b, updated_variance_b = adaptive_update(central_up_matrix, running_mean_up, squared_average_up, gradient_b)
    updated_factor_a, updated_moment_a, updated_variance_a = adaptive_update(central_down_matrix, running_mean_down, squared_average_down, gradient_a)
    thin_up_matrix = updated_factor_b.astype(jnp.bfloat16)
    lowrank_a = updated_factor_a.astype(jnp.bfloat16)
    tile_lines = math.gcd(EMBED_SPAN, 512)
    partition_list = EMBED_SPAN // tile_lines

    def submatrix_piece(pieces):
        codes, scales, left_product = pieces
        decode_weight = decode(codes) * scales[:, None]
        merged_weight = decode_weight + adapter_scale * jnp.dot(left_product, lowrank_a, preferred_element_type=jnp.float32)
        peak = lax.optimization_barrier(jnp.max(jnp.abs(merged_weight), axis=1)) + peak_eps
        return ((merged_weight / peak[:, None]).astype(jnp.bfloat16), peak / fp8_top)
    combined_normalized_entries, fresh_line_multipliers = lax.map(submatrix_piece, (fixed_matrix_encodings.reshape(partition_list, tile_lines, INNER_NEURONS), line_restore_multiplier.reshape(partition_list, tile_lines), thin_up_matrix.reshape(partition_list, tile_lines, ADAPT_DIMENSION)))
    return (combined_normalized_entries.reshape(EMBED_SPAN, INNER_NEURONS), fresh_line_multipliers.reshape(EMBED_SPAN), updated_factor_b, updated_factor_a, updated_moment_b, updated_variance_b, updated_moment_a, updated_variance_a)
```

```python
import functools

import jax
import jax.numpy as jnp
from jax import lax
from jax.experimental import pallas as pl
from jax.experimental.pallas import tpu as pltpu
from jax.sharding import PartitionSpec as P

first_decay = 0.9
second_decay = 0.99
server_rate = 0.1
adam_floor = 0.001
adapter_scale = 2.0
count_scale = 64.0
fp8_top = 448.0
peak_eps = 1e-06
MESH = pl.DeviceIdType.MESH
LANES = 128
decode_lines = 32
merge_lines = 128
code_slots = 3


def tile_of(width, limit):
    best = LANES
    for tile in range(LANES, limit + 1, LANES):
        if width % tile == 0:
            best = tile
    return best


def adaptive_update(param, moment, second, grad):
    moment_next = first_decay * moment + (1.0 - first_decay) * grad
    second_next = second_decay * second + (1.0 - second_decay) * grad * grad
    param_next = param - server_rate * moment_next / (jnp.sqrt(second_next) + adam_floor)
    return (param_next, moment_next, second_next)


def scaled_decode(codes):
    low = codes & 127
    mantissa = codes & 7
    mantissa = jnp.where(low > 7, mantissa | 8, mantissa)
    magnitude = mantissa << jnp.maximum(low >> 3, 1)
    return jnp.where(codes > 127, -magnitude, magnitude).astype(jnp.float32)


def merge_kernel(
    rows_count, cols_count,
    codes, scale, pb, mb, vb, pa, ma, va, delta_b, delta_a, weight,
    merged, peak_wide, peak_out, nb, nmb, nvb, na, nma, nva,
    dense, code_buf, got_b, got_a, got_w, fac_b, fac_a, all_b, all_a, wide_b, wide_a,
    left, right, scale_wide, top, top_send, got_top,
    code_sem, out_sem, send_sem, recv_sem, gather_send, gather_recv, own_sem,
):
    my_row, my_col = lax.axis_index("row"), lax.axis_index("col")
    count = rows_count * cols_count
    me = my_row * cols_count + my_col
    depth, width = dense.shape
    steps = depth // decode_lines
    tile = tile_of(width, 1024)
    tiles = width // tile
    rank_b, rank_a = pb.shape[0], pa.shape[0]

    def fetch(i):
        slot = lax.rem(i, code_slots)
        return pltpu.make_async_copy(
            codes.at[pl.ds(i * decode_lines, decode_lines)], code_buf.at[slot], code_sem.at[slot]
        )

    for i in range(code_slots):
        fetch(i).start()

    barrier = pltpu.get_barrier_semaphore()

    def greet(k, _):
        to = lax.rem(me + k, count)
        pl.semaphore_signal(
            barrier, inc=1, device_id=(to // cols_count, lax.rem(to, cols_count)), device_id_type=MESH
        )
        return 0

    lax.fori_loop(1, count, greet, 0)
    pl.semaphore_wait(barrier, count - 1)

    def block_a(row, col):
        return delta_a.at[row, :, pl.ds(pl.multiple_of(col * width, LANES), width)]

    def block_b(row, col):
        return delta_b.at[col, :, pl.ds(pl.multiple_of(row * depth, LANES), depth)]

    def exchange(to, source):
        row, col = to // cols_count, lax.rem(to, cols_count)
        parts = (
            (weight, got_w.at[source]),
            (block_b(row, col), got_b.at[source]),
            (block_a(row, col), got_a.at[source]),
        )
        return [
            pltpu.make_async_remote_copy(
                src_ref=src, dst_ref=dst, send_sem=send_sem.at[n, to], recv_sem=recv_sem.at[n, source],
                device_id=(row, col), device_id_type=MESH,
            )
            for n, (src, dst) in enumerate(parts)
        ]

    def send(k, _):
        for copy in exchange(lax.rem(me + k, count), me):
            copy.start()
        return 0

    lax.fori_loop(1, count, send, 0)
    own = [
        pltpu.make_async_copy(weight, got_w.at[me], own_sem.at[0]),
        pltpu.make_async_copy(block_b(my_row, my_col), got_b.at[me], own_sem.at[1]),
        pltpu.make_async_copy(block_a(my_row, my_col), got_a.at[me], own_sem.at[2]),
    ]
    for copy in own:
        copy.start()

    for b in range(depth // LANES):
        line = jnp.broadcast_to(scale[b : b + 1, :] * 2.0 ** (-10), (LANES, LANES))
        scale_wide[b * LANES : (b + 1) * LANES, :] = line.T

    def decode_step(i, _):
        slot = lax.rem(i, code_slots)
        fetch(i).wait()

        def column(j, _):
            at = pl.ds(pl.multiple_of(j * tile, LANES), tile)
            for g in range(decode_lines // 16):
                value = scaled_decode(code_buf[slot, g * 16 : (g + 1) * 16, at])
                dense[pl.ds(pl.multiple_of(i * decode_lines + g * 16, 16), 16), at] = value.astype(
                    jnp.bfloat16
                )
            return 0

        lax.fori_loop(0, tiles, column, 0)

        @pl.when(i + code_slots < steps)
        def _():
            fetch(i + code_slots).start()

        return 0

    lax.fori_loop(0, steps, decode_step, 0)

    for copy in own:
        copy.wait()

    def arrive(k, _):
        source = lax.rem(me + k, count)
        for copy in exchange(source, source):
            copy.wait_recv()
        return 0

    lax.fori_loop(1, count, arrive, 0)

    def summed(got, which, at, shape):
        def add(s, total):
            return total + got_w[s, which : which + 1, 0:1] * got[s, :, at].astype(jnp.float32)

        return lax.fori_loop(0, count, add, jnp.zeros(shape, jnp.float32), unroll=8)

    grad_b = summed(got_b, 0, slice(None), (rank_b, depth))
    p, m, v = adaptive_update(pb[...], mb[...], vb[...], grad_b)
    nb[...] = p
    nmb[...] = m
    nvb[...] = v
    fac_b[...] = p.astype(jnp.bfloat16)

    def gather_b(to, source):
        return pltpu.make_async_remote_copy(
            src_ref=fac_b, dst_ref=all_b.at[source], send_sem=gather_send.at[0, to],
            recv_sem=gather_recv.at[0, source], device_id=(my_row, to), device_id_type=MESH,
        )

    def gather_a(to, source):
        return pltpu.make_async_remote_copy(
            src_ref=fac_a, dst_ref=all_a.at[source], send_sem=gather_send.at[1, to],
            recv_sem=gather_recv.at[1, source], device_id=(to, my_col), device_id_type=MESH,
        )

    for k in range(1, cols_count):
        gather_b(lax.rem(my_col + k, cols_count), my_col).start()
    own_b = pltpu.make_async_copy(fac_b, all_b.at[my_col], own_sem.at[0])
    own_b.start()

    def update_a(j, _):
        at = pl.ds(pl.multiple_of(j * tile, LANES), tile)
        grad = summed(got_a, 1, at, (rank_a, tile))
        p, m, v = adaptive_update(pa[:, at], ma[:, at], va[:, at], grad)
        na[:, at] = p
        nma[:, at] = m
        nva[:, at] = v
        fac_a[:, at] = p.astype(jnp.bfloat16)
        return 0

    lax.fori_loop(0, tiles, update_a, 0)
    for k in range(1, rows_count):
        gather_a(lax.rem(my_row + k, rows_count), my_row).start()
    own_a = pltpu.make_async_copy(fac_a, all_a.at[my_row], own_sem.at[1])
    own_a.start()

    own_b.wait()
    for k in range(1, cols_count):
        source = lax.rem(my_col + k, cols_count)
        gather_b(source, source).wait_recv()
    for c in range(cols_count):
        wide_b[c * rank_b : (c + 1) * rank_b, :] = all_b[c].astype(jnp.float32)
    left[...] = wide_b[...].T.astype(jnp.bfloat16)

    own_a.wait()
    for k in range(1, rows_count):
        source = lax.rem(my_row + k, rows_count)
        gather_a(source, source).wait_recv()

    def assemble(j, _):
        at = pl.ds(pl.multiple_of(j * tile, LANES), tile)
        for r in range(rows_count):
            wide_a[r * rank_a : (r + 1) * rank_a, :] = all_a[r, :, at].astype(jnp.float32)
        right[:, at] = wide_a[...].astype(jnp.bfloat16)
        return 0

    lax.fori_loop(0, tiles, assemble, 0)

    def put(i):
        lines = pl.ds(pl.multiple_of(i * merge_lines, merge_lines), merge_lines)
        return pltpu.make_async_copy(dense.at[lines], merged.at[lines], out_sem.at[i])

    def merge_step(i, _):
        lines = pl.ds(pl.multiple_of(i * merge_lines, merge_lines), merge_lines)
        top[lines, :] = jnp.zeros((merge_lines, LANES), jnp.float32)

        def column(j, _):
            at = pl.ds(pl.multiple_of(j * tile, LANES), tile)
            product = jnp.dot(left[lines, :], right[:, at], preferred_element_type=jnp.float32)
            for g in range(merge_lines // 16):
                group = pl.ds(pl.multiple_of(i * merge_lines + g * 16, 16), 16)
                line_scale = scale_wide[group, :]
                highest = top[group, :]
                for t in range(tile // LANES):
                    lane = pl.ds(pl.multiple_of(j * tile + t * LANES, LANES), LANES)
                    value = dense[group, lane].astype(jnp.float32) * line_scale
                    value = value + adapter_scale * product[
                        g * 16 : (g + 1) * 16, t * LANES : (t + 1) * LANES
                    ]
                    highest = jnp.maximum(highest, jnp.abs(value))
                    dense[group, lane] = value.astype(jnp.bfloat16)
                top[group, :] = highest
            return 0

        lax.fori_loop(0, tiles, column, 0)
        put(i).start()
        return 0

    lax.fori_loop(0, depth // merge_lines, merge_step, 0)

    for b in range(depth // LANES):
        square = top[b * LANES : (b + 1) * LANES, :]
        top_send[b : b + 1, :] = jnp.max(square.T, axis=0, keepdims=True)

    def gather_top(to, source):
        return pltpu.make_async_remote_copy(
            src_ref=top_send, dst_ref=got_top.at[source], send_sem=gather_send.at[2, to],
            recv_sem=gather_recv.at[2, source], device_id=(my_row, to), device_id_type=MESH,
        )

    for k in range(1, cols_count):
        gather_top(lax.rem(my_col + k, cols_count), my_col).start()
    peak = top_send[...]
    for k in range(1, cols_count):
        source = lax.rem(my_col + k, cols_count)
        gather_top(source, source).wait_recv()
        peak = jnp.maximum(peak, got_top[source])
    peak = peak + peak_eps
    peak_out[...] = peak / fp8_top
    for b in range(depth // LANES):
        peak_wide[b * LANES : (b + 1) * LANES, :] = jnp.broadcast_to(
            1.0 / peak[b : b + 1, :], (LANES, LANES)
        ).T

    def drain(i, _):
        put(i).wait()
        return 0

    lax.fori_loop(0, depth // merge_lines, drain, 0)

    def sent(k, _):
        for copy in exchange(lax.rem(me + k, count), me):
            copy.wait_send()
        return 0

    lax.fori_loop(1, count, sent, 0)
    for k in range(1, cols_count):
        to = lax.rem(my_col + k, cols_count)
        gather_b(to, my_col).wait_send()
        gather_top(to, my_col).wait_send()
    for k in range(1, rows_count):
        gather_a(lax.rem(my_row + k, rows_count), my_row).wait_send()


def normalize_kernel(merged, inverse, out):
    for t in range(merged.shape[1] // LANES):
        at = slice(t * LANES, (t + 1) * LANES)
        out[:, at] = (merged[:, at].astype(jnp.float32) * inverse[...]).astype(jnp.bfloat16)


def local(
    fixed_matrix_encodings,
    line_restore_multiplier,
    central_up_matrix,
    central_down_matrix,
    running_mean_up,
    squared_average_up,
    running_mean_down,
    squared_average_down,
    participant_change_up,
    participant_change_down,
    client_tallies,
):
    rows_count = lax.axis_size("row")
    cols_count = lax.axis_size("col")
    count = rows_count * cols_count
    depth, width = fixed_matrix_encodings.shape
    rank_b = central_up_matrix.shape[1]
    rank_a = central_down_matrix.shape[0]
    rank = participant_change_down.shape[1]
    blocks = depth // LANES
    everyone = client_tallies.shape[0] * count
    weights = client_tallies.astype(jnp.float32) / (count_scale * everyone)
    weight = jnp.broadcast_to(weights[0][:, None], (2, LANES))
    delta_b = participant_change_up[0].T.reshape(cols_count, rank_b, depth * rows_count)
    delta_a = participant_change_down[0].reshape(rows_count, rank_a, width * cols_count)
    anywhere = pl.BlockSpec(memory_space=pl.ANY)
    vmem = pl.BlockSpec(memory_space=pltpu.VMEM)
    f32, bf16 = jnp.float32, jnp.bfloat16
    shape = jax.ShapeDtypeStruct
    outs = pl.pallas_call(
        functools.partial(merge_kernel, rows_count, cols_count),
        out_shape=[
            shape((depth, width), bf16),
            shape((depth, LANES), f32),
            shape((blocks, LANES), f32),
        ]
        + [shape((rank_b, depth), f32)] * 3
        + [shape((rank_a, width), f32)] * 3,
        in_specs=[anywhere] + [vmem] * 7 + [anywhere] * 2 + [vmem],
        out_specs=[anywhere] + [vmem] * 8,
        scratch_shapes=[
            pltpu.VMEM((depth, width), bf16),
            pltpu.VMEM((code_slots, decode_lines, width), jnp.int32),
            pltpu.VMEM((count, rank_b, depth), bf16),
            pltpu.VMEM((count, rank_a, width), bf16),
            pltpu.VMEM((count, 2, LANES), f32),
            pltpu.VMEM((rank_b, depth), bf16),
            pltpu.VMEM((rank_a, width), bf16),
            pltpu.VMEM((cols_count, rank_b, depth), bf16),
            pltpu.VMEM((rows_count, rank_a, width), bf16),
            pltpu.VMEM((rank, depth), f32),
            pltpu.VMEM((rank, tile_of(width, 1024)), f32),
            pltpu.VMEM((depth, rank), bf16),
            pltpu.VMEM((rank, width), bf16),
            pltpu.VMEM((depth, LANES), f32),
            pltpu.VMEM((depth, LANES), f32),
            pltpu.VMEM((blocks, LANES), f32),
            pltpu.VMEM((cols_count, blocks, LANES), f32),
            pltpu.SemaphoreType.DMA((code_slots,)),
            pltpu.SemaphoreType.DMA((depth // merge_lines,)),
            pltpu.SemaphoreType.DMA((3, count)),
            pltpu.SemaphoreType.DMA((3, count)),
            pltpu.SemaphoreType.DMA((3, max(rows_count, cols_count))),
            pltpu.SemaphoreType.DMA((3, max(rows_count, cols_count))),
            pltpu.SemaphoreType.DMA((3,)),
        ],
        compiler_params=pltpu.CompilerParams(
            collective_id=0, has_side_effects=True, vmem_limit_bytes=62_000_000
        ),
    )(
        fixed_matrix_encodings,
        line_restore_multiplier.reshape(blocks, LANES),
        central_up_matrix.T,
        running_mean_up.T,
        squared_average_up.T,
        central_down_matrix,
        running_mean_down,
        squared_average_down,
        delta_b,
        delta_a,
        weight,
    )
    merged, inverse, fresh, nb, nmb, nvb, na, nma, nva = outs
    step = 64
    normalized = pl.pallas_call(
        normalize_kernel,
        grid=(depth // step,),
        out_shape=shape((depth, width), bf16),
        in_specs=[
            pl.BlockSpec((step, width), lambda i: (i, 0)),
            pl.BlockSpec((step, LANES), lambda i: (i, 0)),
        ],
        out_specs=pl.BlockSpec((step, width), lambda i: (i, 0)),
    )(merged, inverse)
    return (normalized, fresh.reshape(depth), nb.T, na, nmb.T, nvb.T, nma, nva)


def solution(mesh):
    grid = P("row", "col")
    clients = P(("row", "col"), None, None)
    return jax.shard_map(
        local,
        mesh=mesh,
        in_specs=(grid, P("row"), grid, grid, grid, grid, grid, grid, clients, clients, P(("row", "col"), None)),
        out_specs=(grid, P("row"), grid, grid, grid, grid, grid, grid),
        check_vma=False,
    )
```

```python
import functools

import jax
import jax.numpy as jnp
from jax import lax
from jax.experimental import pallas as pl
from jax.experimental.pallas import tpu as pltpu
from jax.sharding import PartitionSpec as P

first_decay = 0.9
second_decay = 0.99
server_rate = 0.1
adam_floor = 0.001
adapter_scale = 2.0
count_scale = 64.0
fp8_top = 448.0
peak_eps = 1e-06
MESH = pl.DeviceIdType.MESH
LANES = 128
decode_lines = 32
merge_lines = 128
code_slots = 3
stage_slots = 2


def tile_of(width, limit):
    best = LANES
    for tile in range(LANES, limit + 1, LANES):
        if width % tile == 0:
            best = tile
    return best


def adaptive_update(param, moment, second, grad):
    moment_next = first_decay * moment + (1.0 - first_decay) * grad
    second_next = second_decay * second + (1.0 - second_decay) * grad * grad
    param_next = param - server_rate * moment_next / (jnp.sqrt(second_next) + adam_floor)
    return (param_next, moment_next, second_next)


def scaled_decode(codes):
    low = codes & 127
    mantissa = codes & 7
    mantissa = jnp.where(low > 7, mantissa | 8, mantissa)
    magnitude = mantissa << jnp.maximum(low >> 3, 1)
    return jnp.where(codes > 127, -magnitude, magnitude).astype(jnp.float32)


def merge_kernel(
    rows_count, cols_count,
    codes, scale, pb, mb, vb, pa, ma, va, delta_b, delta_a, weight,
    merged, peak_wide, peak_out, nb, nmb, nvb, na, nma, nva,
    dense, code_buf, got_b, got_a, got_w, fac_b, fac_a, all_b, all_a, wide_b, wide_a,
    left, right, stage, scale_wide, top, top_send, got_top,
    code_sem, out_sem, send_sem, recv_sem, gather_send, gather_recv, own_sem,
):
    my_row, my_col = lax.axis_index("row"), lax.axis_index("col")
    count = rows_count * cols_count
    me = my_row * cols_count + my_col
    depth, width = dense.shape
    steps = depth // decode_lines
    tile = tile_of(width, 1024)
    tiles = width // tile
    rank_b, rank_a = pb.shape[0], pa.shape[0]

    def fetch(i):
        slot = lax.rem(i, code_slots)
        return pltpu.make_async_copy(
            codes.at[pl.ds(i * decode_lines, decode_lines)], code_buf.at[slot], code_sem.at[slot]
        )

    for i in range(code_slots):
        fetch(i).start()

    barrier = pltpu.get_barrier_semaphore()

    def greet(k, _):
        to = lax.rem(me + k, count)
        pl.semaphore_signal(
            barrier, inc=1, device_id=(to // cols_count, lax.rem(to, cols_count)), device_id_type=MESH
        )
        return 0

    lax.fori_loop(1, count, greet, 0)
    pl.semaphore_wait(barrier, count - 1)

    def block_a(row, col):
        return delta_a.at[row, :, pl.ds(pl.multiple_of(col * width, LANES), width)]

    def block_b(row, col):
        return delta_b.at[col, :, pl.ds(pl.multiple_of(row * depth, LANES), depth)]

    def exchange(to, source):
        row, col = to // cols_count, lax.rem(to, cols_count)
        parts = (
            (weight, got_w.at[source]),
            (block_b(row, col), got_b.at[source]),
            (block_a(row, col), got_a.at[source]),
        )
        return [
            pltpu.make_async_remote_copy(
                src_ref=src, dst_ref=dst, send_sem=send_sem.at[n, to], recv_sem=recv_sem.at[n, source],
                device_id=(row, col), device_id_type=MESH,
            )
            for n, (src, dst) in enumerate(parts)
        ]

    def send(k, _):
        for copy in exchange(lax.rem(me + k, count), me):
            copy.start()
        return 0

    lax.fori_loop(1, count, send, 0)
    own = [
        pltpu.make_async_copy(weight, got_w.at[me], own_sem.at[0]),
        pltpu.make_async_copy(block_b(my_row, my_col), got_b.at[me], own_sem.at[1]),
        pltpu.make_async_copy(block_a(my_row, my_col), got_a.at[me], own_sem.at[2]),
    ]
    for copy in own:
        copy.start()

    for b in range(depth // LANES):
        line = jnp.broadcast_to(scale[b : b + 1, :] * 2.0 ** (-10), (LANES, LANES))
        scale_wide[b * LANES : (b + 1) * LANES, :] = line.T

    def decode_step(i, _):
        slot = lax.rem(i, code_slots)
        fetch(i).wait()

        def column(j, _):
            at = pl.ds(pl.multiple_of(j * tile, LANES), tile)
            for g in range(decode_lines // 16):
                value = scaled_decode(code_buf[slot, g * 16 : (g + 1) * 16, at])
                dense[pl.ds(pl.multiple_of(i * decode_lines + g * 16, 16), 16), at] = value.astype(
                    jnp.bfloat16
                )
            return 0

        lax.fori_loop(0, tiles, column, 0)

        @pl.when(i + code_slots < steps)
        def _():
            fetch(i + code_slots).start()

        return 0

    lax.fori_loop(0, steps, decode_step, 0)

    for copy in own:
        copy.wait()

    def arrive(k, _):
        source = lax.rem(me + k, count)
        for copy in exchange(source, source):
            copy.wait_recv()
        return 0

    lax.fori_loop(1, count, arrive, 0)

    def summed(got, which, at, shape):
        def add(s, total):
            return total + got_w[s, which : which + 1, 0:1] * got[s, :, at].astype(jnp.float32)

        return lax.fori_loop(0, count, add, jnp.zeros(shape, jnp.float32), unroll=8)

    grad_b = summed(got_b, 0, slice(None), (rank_b, depth))
    p, m, v = adaptive_update(pb[...], mb[...], vb[...], grad_b)
    nb[...] = p
    nmb[...] = m
    nvb[...] = v
    fac_b[...] = p.astype(jnp.bfloat16)

    def gather_b(to, source):
        return pltpu.make_async_remote_copy(
            src_ref=fac_b, dst_ref=all_b.at[source], send_sem=gather_send.at[0, to],
            recv_sem=gather_recv.at[0, source], device_id=(my_row, to), device_id_type=MESH,
        )

    def gather_a(to, source):
        return pltpu.make_async_remote_copy(
            src_ref=fac_a, dst_ref=all_a.at[source], send_sem=gather_send.at[1, to],
            recv_sem=gather_recv.at[1, source], device_id=(to, my_col), device_id_type=MESH,
        )

    for k in range(1, cols_count):
        gather_b(lax.rem(my_col + k, cols_count), my_col).start()
    own_b = pltpu.make_async_copy(fac_b, all_b.at[my_col], own_sem.at[0])
    own_b.start()

    def update_a(j, _):
        at = pl.ds(pl.multiple_of(j * tile, LANES), tile)
        grad = summed(got_a, 1, at, (rank_a, tile))
        p, m, v = adaptive_update(pa[:, at], ma[:, at], va[:, at], grad)
        na[:, at] = p
        nma[:, at] = m
        nva[:, at] = v
        fac_a[:, at] = p.astype(jnp.bfloat16)
        return 0

    lax.fori_loop(0, tiles, update_a, 0)
    for k in range(1, rows_count):
        gather_a(lax.rem(my_row + k, rows_count), my_row).start()
    own_a = pltpu.make_async_copy(fac_a, all_a.at[my_row], own_sem.at[1])
    own_a.start()

    own_b.wait()
    for k in range(1, cols_count):
        source = lax.rem(my_col + k, cols_count)
        gather_b(source, source).wait_recv()
    for c in range(cols_count):
        wide_b[c * rank_b : (c + 1) * rank_b, :] = all_b[c].astype(jnp.float32)
    left[...] = wide_b[...].T.astype(jnp.bfloat16)

    own_a.wait()
    for k in range(1, rows_count):
        source = lax.rem(my_row + k, rows_count)
        gather_a(source, source).wait_recv()

    def assemble(j, _):
        at = pl.ds(pl.multiple_of(j * tile, LANES), tile)
        for r in range(rows_count):
            wide_a[r * rank_a : (r + 1) * rank_a, :] = all_a[r, :, at].astype(jnp.float32)
        right[:, at] = wide_a[...].astype(jnp.bfloat16)
        return 0

    lax.fori_loop(0, tiles, assemble, 0)

    def put(i):
        slot = lax.rem(i, stage_slots)
        lines = pl.ds(pl.multiple_of(i * merge_lines, merge_lines), merge_lines)
        return pltpu.make_async_copy(stage.at[slot], merged.at[lines], out_sem.at[slot])

    merge_steps = depth // merge_lines

    def merge_step(i, _):
        slot = lax.rem(i, stage_slots)
        lines = pl.ds(pl.multiple_of(i * merge_lines, merge_lines), merge_lines)

        @pl.when(i >= stage_slots)
        def _():
            put(i - stage_slots).wait()

        factor = left[lines, :]
        line_scale = scale_wide[lines, :]

        def column(j, highest):
            for t in range(tile // LANES):
                lane = pl.ds(pl.multiple_of(j * tile + t * LANES, LANES), LANES)
                product = jnp.dot(factor, right[:, lane], preferred_element_type=jnp.float32)
                value = dense[lines, lane].astype(jnp.float32) * line_scale
                value = value + adapter_scale * product
                highest = jnp.maximum(highest, jnp.abs(value))
                stage[slot, :, lane] = value.astype(jnp.bfloat16)
            return highest

        top[lines, :] = lax.fori_loop(
            0, tiles, column, jnp.zeros((merge_lines, LANES), jnp.float32)
        )
        put(i).start()
        return 0

    lax.fori_loop(0, merge_steps, merge_step, 0)

    for b in range(depth // LANES):
        square = top[b * LANES : (b + 1) * LANES, :]
        top_send[b : b + 1, :] = jnp.max(square.T, axis=0, keepdims=True)

    def gather_top(to, source):
        return pltpu.make_async_remote_copy(
            src_ref=top_send, dst_ref=got_top.at[source], send_sem=gather_send.at[2, to],
            recv_sem=gather_recv.at[2, source], device_id=(my_row, to), device_id_type=MESH,
        )

    for k in range(1, cols_count):
        gather_top(lax.rem(my_col + k, cols_count), my_col).start()
    peak = top_send[...]
    for k in range(1, cols_count):
        source = lax.rem(my_col + k, cols_count)
        gather_top(source, source).wait_recv()
        peak = jnp.maximum(peak, got_top[source])
    peak = peak + peak_eps
    peak_out[...] = peak / fp8_top
    for b in range(depth // LANES):
        peak_wide[b * LANES : (b + 1) * LANES, :] = jnp.broadcast_to(
            1.0 / peak[b : b + 1, :], (LANES, LANES)
        ).T

    def drain(i, _):
        put(i).wait()
        return 0

    lax.fori_loop(merge_steps - stage_slots, merge_steps, drain, 0)

    def sent(k, _):
        for copy in exchange(lax.rem(me + k, count), me):
            copy.wait_send()
        return 0

    lax.fori_loop(1, count, sent, 0)
    for k in range(1, cols_count):
        to = lax.rem(my_col + k, cols_count)
        gather_b(to, my_col).wait_send()
        gather_top(to, my_col).wait_send()
    for k in range(1, rows_count):
        gather_a(lax.rem(my_row + k, rows_count), my_row).wait_send()


def normalize_kernel(merged, inverse, out):
    for t in range(merged.shape[1] // LANES):
        at = slice(t * LANES, (t + 1) * LANES)
        out[:, at] = (merged[:, at].astype(jnp.float32) * inverse[...]).astype(jnp.bfloat16)


def local(
    fixed_matrix_encodings,
    line_restore_multiplier,
    central_up_matrix,
    central_down_matrix,
    running_mean_up,
    squared_average_up,
    running_mean_down,
    squared_average_down,
    participant_change_up,
    participant_change_down,
    client_tallies,
):
    rows_count = lax.axis_size("row")
    cols_count = lax.axis_size("col")
    count = rows_count * cols_count
    depth, width = fixed_matrix_encodings.shape
    rank_b = central_up_matrix.shape[1]
    rank_a = central_down_matrix.shape[0]
    rank = participant_change_down.shape[1]
    blocks = depth // LANES
    everyone = client_tallies.shape[0] * count
    weights = client_tallies.astype(jnp.float32) / (count_scale * everyone)
    weight = jnp.broadcast_to(weights[0][:, None], (2, LANES))
    delta_b = participant_change_up[0].T.reshape(cols_count, rank_b, depth * rows_count)
    delta_a = participant_change_down[0].reshape(rows_count, rank_a, width * cols_count)
    anywhere = pl.BlockSpec(memory_space=pl.ANY)
    vmem = pl.BlockSpec(memory_space=pltpu.VMEM)
    f32, bf16 = jnp.float32, jnp.bfloat16
    shape = jax.ShapeDtypeStruct
    outs = pl.pallas_call(
        functools.partial(merge_kernel, rows_count, cols_count),
        out_shape=[
            shape((depth, width), bf16),
            shape((depth, LANES), f32),
            shape((blocks, LANES), f32),
        ]
        + [shape((rank_b, depth), f32)] * 3
        + [shape((rank_a, width), f32)] * 3,
        in_specs=[anywhere] + [vmem] * 7 + [anywhere] * 2 + [vmem],
        out_specs=[anywhere] + [vmem] * 8,
        scratch_shapes=[
            pltpu.VMEM((depth, width), bf16),
            pltpu.VMEM((code_slots, decode_lines, width), jnp.int32),
            pltpu.VMEM((count, rank_b, depth), bf16),
            pltpu.VMEM((count, rank_a, width), bf16),
            pltpu.VMEM((count, 2, LANES), f32),
            pltpu.VMEM((rank_b, depth), bf16),
            pltpu.VMEM((rank_a, width), bf16),
            pltpu.VMEM((cols_count, rank_b, depth), bf16),
            pltpu.VMEM((rows_count, rank_a, width), bf16),
            pltpu.VMEM((rank, depth), f32),
            pltpu.VMEM((rank, tile_of(width, 1024)), f32),
            pltpu.VMEM((depth, rank), bf16),
            pltpu.VMEM((rank, width), bf16),
            pltpu.VMEM((stage_slots, merge_lines, width), bf16),
            pltpu.VMEM((depth, LANES), f32),
            pltpu.VMEM((depth, LANES), f32),
            pltpu.VMEM((blocks, LANES), f32),
            pltpu.VMEM((cols_count, blocks, LANES), f32),
            pltpu.SemaphoreType.DMA((code_slots,)),
            pltpu.SemaphoreType.DMA((stage_slots,)),
            pltpu.SemaphoreType.DMA((3, count)),
            pltpu.SemaphoreType.DMA((3, count)),
            pltpu.SemaphoreType.DMA((3, max(rows_count, cols_count))),
            pltpu.SemaphoreType.DMA((3, max(rows_count, cols_count))),
            pltpu.SemaphoreType.DMA((3,)),
        ],
        compiler_params=pltpu.CompilerParams(
            collective_id=0, has_side_effects=True, vmem_limit_bytes=62_000_000
        ),
    )(
        fixed_matrix_encodings,
        line_restore_multiplier.reshape(blocks, LANES),
        central_up_matrix.T,
        running_mean_up.T,
        squared_average_up.T,
        central_down_matrix,
        running_mean_down,
        squared_average_down,
        delta_b,
        delta_a,
        weight,
    )
    merged, inverse, fresh, nb, nmb, nvb, na, nma, nva = outs
    step = 64
    normalized = pl.pallas_call(
        normalize_kernel,
        grid=(depth // step,),
        out_shape=shape((depth, width), bf16),
        in_specs=[
            pl.BlockSpec((step, width), lambda i: (i, 0)),
            pl.BlockSpec((step, LANES), lambda i: (i, 0)),
        ],
        out_specs=pl.BlockSpec((step, width), lambda i: (i, 0)),
    )(merged, inverse)
    return (normalized, fresh.reshape(depth), nb.T, na, nmb.T, nvb.T, nma, nva)


def solution(mesh):
    grid = P("row", "col")
    clients = P(("row", "col"), None, None)
    return jax.shard_map(
        local,
        mesh=mesh,
        in_specs=(grid, P("row"), grid, grid, grid, grid, grid, grid, clients, clients, P(("row", "col"), None)),
        out_specs=(grid, P("row"), grid, grid, grid, grid, grid, grid),
        check_vma=False,
    )
```
